256 devices in a mesh: dp: 8 (over y, core), expert: 32 (over x, z).
Axes of the slice: x: 4, y: 4, z: 8, core: 2. Of those that a mesh axis runs over, the one named last changes fastest.
Arguments:
- tokens: bfloat16 [2048, 3584], P(('dp', 'expert')), may hold values from -6 to 6
- routes: int32 [2048, 8], P(('dp', 'expert')), may hold values from 0 to 63, all different within a row; in each aligned block of 8 rows (0 to 7, 8 to 15, ...) at most 2 rows name the same one
- gates: bfloat16 [2048, 8], P(('dp', 'expert')), may hold values from 0.049804688 to 0.5
- cotangent: bfloat16 [2048, 3584], P(('dp', 'expert')), may hold values from -1.5 to 1.5
- w_gate: bfloat16 [64, 3584, 1024], P('expert', None, 'dp'), may hold values from -0.09375 to 0.09375
- w_up: bfloat16 [64, 3584, 1024], P('expert', None, 'dp'), may hold values from -0.09375 to 0.09375
- w_down: bfloat16 [64, 1024, 3584], P('expert', 'dp'), may hold values from -0.1875 to 0.1875
Outputs:
- token_grads: bfloat16 [2048, 3584], P(('dp', 'expert'))
- gate_grads: float32 [2048, 8], P(('dp', 'expert'))
- grad_gate: bfloat16 [64, 3584, 1024], P('expert', None, 'dp')
- grad_up: bfloat16 [64, 3584, 1024], P('expert', None, 'dp')
- grad_down: bfloat16 [64, 1024, 3584], P('expert', 'dp')
The draws below stay inside these ranges and needn't reach their ends.
Inputs may be any that keep to these rules, and one draw needn't show every extreme that they name: `routes`: each row names 8 different experts. Within each device's block of 8 rows no expert is named by more than 2 rows, a bound that some block reaches.
All inputs are finite; a program needn't handle non-finite values.
Results may differ from the reference program's by a relative error of at most 0.0058.
Values may be sent and summed in bfloat16 or wider, within the bound.
A program may use at most 192 MiB of HBM per device.

```python
import math
import jax
import jax.numpy as jnp
import numpy as np
from jax import lax

D = 3584
H = 1024
TOPK = 8
TOK_DEV = 8
EXPERTS = 64
CAP = 2
TOKENS = 2048


def levels(own_key, shape, cuts, least, high):
    factor_of = 1.0
    for position, blocks in cuts:
        heights = jax.random.uniform(jax.random.fold_in(jax.random.fold_in(own_key, 6), position), (blocks,), jnp.float32, least / len(cuts), high / len(cuts))
        factor_of = factor_of * jnp.repeat(jnp.exp(heights), shape[position] // blocks).reshape((-1,) + (1,) * (len(shape) - 1 - position))
    return factor_of


def routed_block(stream_key, own, number, rows, count, top, bound, lean):
    order = jax.random.permutation(stream_key, count)
    packed, ordinary = shares(count, rows * top, bound, lean, True), shares(count, rows * top, bound, lean, False)
    places = jnp.arange(count)

    def named(tallies, rotation):
        used = int((tallies > 0).sum())
        fixed = max(1, used // 4)
        shifted = fixed + (places - fixed + rotation * (used - fixed)) % max(1, count - fixed)
        return jnp.zeros((count,), jnp.int32).at[order[jnp.where(places < fixed, places, shifted)]].set(jnp.asarray(tallies, jnp.int32))

    tallies = jnp.where(number % 4 == 0, named(packed, number // 4), named(ordinary, number - number // 4 - 1))
    mixed = jax.random.permutation(jax.random.fold_in(own, 3), count)
    donor, sink = mixed[0:count // 2 * 2:2], mixed[1:count // 2 * 2:2]
    room = jnp.minimum(tallies[donor] - 1, bound - tallies[sink]) // 2
    room = jnp.where((donor == order[0]) | (sink == order[0]) | (tallies[sink] == 0), 0, jnp.maximum(room, 0))
    shifted = jax.random.randint(jax.random.fold_in(own, 4), (count // 2,), 0, 1 << 20) % (room + 1)
    tallies = tallies.at[donor].add(-shifted).at[sink].add(shifted)
    members = jnp.searchsorted(jnp.cumsum(tallies), jnp.arange(rows * top), side="right").astype(jnp.int32)
    grid = members.reshape(top, rows).T
    grid = grid[jax.random.permutation(jax.random.fold_in(own, 1), rows)]
    rotation = jax.random.randint(jax.random.fold_in(own, 2), (rows, 1), 0, top)
    return jnp.take_along_axis(grid, (jnp.arange(top)[None, :] + rotation) % top, axis=1)


def shares(number_of, total, bound, slope, full):
    weights = [(1 << 20) // math.isqrt(rank ** slope) + 1 for rank in range(1, number_of + 1)]
    largest = bound if full else min(bound, max(-(-total // number_of), total * weights[0] // sum(weights)))
    least = 1 if total - largest >= number_of - 1 else 0
    given, surplus = [largest] + [least] * (number_of - 1), total - largest - least * (number_of - 1)
    while surplus > 0:
        movable = [i for i in range(1, number_of) if given[i] < largest] or [i for i in range(1, number_of) if given[i] < bound]
        pool, budget = sum([weights[i] for i in movable]), surplus
        for i in movable:
            more = min(bound - given[i], max(1, budget * weights[i] // pool), surplus)
            given[i] = given[i] + more
            surplus = surplus - more
    return np.array(given)


def bell_draw(key, extent, scale, bound, pieces=(), kind=jnp.bfloat16):
    factor_of = levels(key, extent, pieces, -0.22, 0.18) if pieces else 1.0
    drawn = jax.random.normal(key, extent, jnp.float32) * scale * factor_of
    return jnp.minimum(jnp.maximum(drawn, -bound), bound).astype(kind)


def setup_inputs(seed: int = 0) -> dict:
    keys = jax.random.split(jax.random.key(seed), 8)
    tokens = bell_draw(keys[0], (TOKENS, D), 1.0, 6.0, ((0, 256),))
    routes_keys = jax.random.split(jax.random.fold_in(keys[1], 1), TOKENS // TOK_DEV)
    routes_turns = jax.random.permutation(jax.random.fold_in(keys[1], 3), TOKENS // TOK_DEV)
    routes = jax.vmap(lambda own, number: routed_block(jax.random.fold_in(keys[1], 2), own, number, TOK_DEV, EXPERTS, TOPK, CAP, 2))(routes_keys, routes_turns).reshape((TOKENS, TOPK))
    gates = jnp.clip(0.049804688 + 0.4501953 * jax.random.uniform(keys[2], (TOKENS, TOPK), jnp.float32) ** levels(keys[2], (TOKENS, TOPK), ((0, 256),), -0.2, 0.2), 0.049804688, 0.5).astype(jnp.bfloat16)
    cotangent = bell_draw(keys[3], (TOKENS, D), 0.25, 1.5, ((0, 256),))
    w_gate = bell_draw(keys[4], (EXPERTS, D, H), D ** -0.5, 0.09375, ((0, 32), (2, 8)))
    w_up = bell_draw(keys[5], (EXPERTS, D, H), D ** -0.5, 0.09375, ((0, 32), (2, 8)))
    w_down = bell_draw(keys[6], (EXPERTS, H, D), H ** -0.5, 0.1875, ((0, 32), (1, 8)))
    return {"tokens": tokens, "routes": routes, "gates": gates, "cotangent": cotangent, "w_gate": w_gate, "w_up": w_up, "w_down": w_down}


def product(left, right):
    return jnp.dot(left, right, precision=lax.Precision.HIGHEST)


def rounded(value):
    return lax.optimization_barrier(value.astype(jnp.bfloat16)).astype(jnp.float32)


def reference(tokens, routes, gates, cotangent, w_gate, w_up, w_down):
    maxrows = (TOKENS // TOK_DEV) * CAP
    token_f = tokens.astype(jnp.float32)
    cot_f = cotangent.astype(jnp.float32)
    gate_f = gates.astype(jnp.float32)
    order = jnp.arange(TOKENS, dtype=jnp.int32)
    limit = jnp.arange(maxrows, dtype=jnp.int32)

    def expert_step(carry, items):
        token_sum, gate_sum = carry
        number, weight_gate, weight_up, weight_down = items
        weight_gate = weight_gate.astype(jnp.float32)
        weight_up = weight_up.astype(jnp.float32)
        weight_down = weight_down.astype(jnp.float32)
        hit = routes == number
        chosen = jnp.any(hit, axis=1)
        weight = jnp.sum(jnp.where(hit, gate_f, 0.0), axis=1)
        place = jnp.cumsum(chosen.astype(jnp.int32)) - 1
        target = jnp.where(chosen, place, maxrows).astype(jnp.int32)
        index = jnp.zeros((maxrows,), jnp.int32).at[target].set(order, mode="drop")
        valid = limit < jnp.sum(chosen.astype(jnp.int32))
        rows_in = token_f[index]
        cot_in = cot_f[index]
        row_gate = jnp.where(valid, weight[index], 0.0)
        gate_pre = product(rows_in, weight_gate)
        upper_pre = product(rows_in, weight_up)
        gate_sig = jax.nn.sigmoid(gate_pre)
        active = rounded(gate_pre * gate_sig * upper_pre)
        output = product(active, weight_down)
        gate_part = jnp.sum(cot_in * output, axis=1)
        scaled = rounded(row_gate[:, None] * cot_in)
        grad_active = product(scaled, weight_down.T)
        grad_upper = rounded(grad_active * gate_pre * gate_sig)
        grad_gpre = rounded(grad_active * upper_pre * gate_sig * (1.0 + gate_pre * (1.0 - gate_sig)))
        token_part = product(grad_gpre, weight_gate.T) + product(grad_upper, weight_up.T)
        token_sum = token_sum.at[index].add(jnp.where(valid[:, None], token_part, 0.0))
        row_dot = jnp.zeros((TOKENS,), jnp.float32).at[index].add(jnp.where(valid, gate_part, 0.0))
        gate_sum = gate_sum + jnp.where(hit, row_dot[:, None], 0.0)
        grad_g = product(rows_in.T, grad_gpre).astype(jnp.bfloat16)
        grad_u = product(rows_in.T, grad_upper).astype(jnp.bfloat16)
        grad_d = product(active.T, scaled).astype(jnp.bfloat16)
        return (token_sum, gate_sum), (grad_g, grad_u, grad_d)

    start = (jnp.zeros((TOKENS, D), jnp.float32), jnp.zeros((TOKENS, TOPK), jnp.float32))
    numbers = jnp.arange(EXPERTS, dtype=jnp.int32)
    (token_sum, gate_sum), (grad_gate, grad_up, grad_down) = lax.scan(expert_step, start, (numbers, w_gate, w_up, w_down))
    return token_sum.astype(jnp.bfloat16), gate_sum, grad_gate, grad_up, grad_down
```

```python
from functools import partial

import jax
import jax.numpy as jnp
from jax import lax
from jax.sharding import PartitionSpec as P

TOPK = 8


def route_table(routes, experts_all, capacity):
    pairs = routes.reshape(-1)
    onehot = (pairs[:, None] == jnp.arange(experts_all, dtype=jnp.int32)[None, :]).astype(jnp.int32)
    before = jnp.cumsum(onehot, axis=0) - onehot
    within = jnp.sum(before * onehot, axis=1)
    target = pairs * capacity + within
    slot_ids = jnp.arange(experts_all * capacity, dtype=jnp.int32)
    return (target[:, None] == slot_ids[None, :]).astype(jnp.float32)


def dispatch(table, tokens, cotangent, gates):
    count = tokens.shape[0]
    slots = table.shape[1]
    spread = table.reshape(count, TOPK, slots).sum(axis=1).astype(jnp.bfloat16)
    slot_tokens = jnp.einsum(
        "ts,td->sd", spread, tokens, preferred_element_type=jnp.float32
    ).astype(jnp.bfloat16)
    slot_cot = jnp.einsum(
        "ts,td->sd", spread, cotangent, preferred_element_type=jnp.float32
    ).astype(jnp.bfloat16)
    flat_gates = gates.reshape(-1).astype(jnp.float32)
    slot_gates = jnp.einsum("ps,p->s", table, flat_gates, precision=lax.Precision.HIGHEST).astype(
        jnp.bfloat16
    )
    return (slot_tokens, slot_cot, slot_gates)


def expert_work(slot_tokens, slot_cot, slot_gates, w_gate, w_up, w_down):
    gate_pre = jnp.einsum("rjcd,jdh->rjch", slot_tokens, w_gate, preferred_element_type=jnp.float32)
    upper_pre = jnp.einsum("rjcd,jdh->rjch", slot_tokens, w_up, preferred_element_type=jnp.float32)
    gate_sig = jax.nn.sigmoid(gate_pre)
    active = (gate_pre * gate_sig * upper_pre).astype(jnp.bfloat16)
    output = jnp.einsum("rjch,jhd->rjcd", active, w_down, preferred_element_type=jnp.float32)
    cot_float = slot_cot.astype(jnp.float32)
    gate_part = jnp.sum(output * cot_float, axis=-1)
    scaled = (slot_gates.astype(jnp.float32)[..., None] * cot_float).astype(jnp.bfloat16)
    grad_active = jnp.einsum("rjcd,jhd->rjch", scaled, w_down, preferred_element_type=jnp.float32)
    grad_upper = (grad_active * gate_pre * gate_sig).astype(jnp.bfloat16)
    grad_gpre = (grad_active * upper_pre * gate_sig * (1.0 + gate_pre * (1.0 - gate_sig))).astype(
        jnp.bfloat16
    )
    token_part = jnp.einsum("rjch,jdh->rjcd", grad_gpre, w_gate, preferred_element_type=jnp.float32)
    token_part = token_part + jnp.einsum(
        "rjch,jdh->rjcd", grad_upper, w_up, preferred_element_type=jnp.float32
    )
    grad_g = jnp.einsum(
        "rjcd,rjch->jdh", slot_tokens, grad_gpre, preferred_element_type=jnp.float32
    ).astype(jnp.bfloat16)
    grad_u = jnp.einsum(
        "rjcd,rjch->jdh", slot_tokens, grad_upper, preferred_element_type=jnp.float32
    ).astype(jnp.bfloat16)
    grad_d = jnp.einsum(
        "rjch,rjcd->jhd", active, scaled, preferred_element_type=jnp.float32
    ).astype(jnp.bfloat16)
    return (token_part, gate_part, grad_g, grad_u, grad_d)


def local(tokens, routes, gates, cotangent, w_gate, w_up, w_down):
    n_expert = lax.axis_size("expert")
    n_groups = lax.axis_size("dp")
    local_experts = w_gate.shape[0]
    experts_all = local_experts * n_expert
    tok_count = tokens.shape[0]
    width = tokens.shape[1]
    capacity = 16 * tok_count // experts_all
    slots = experts_all * capacity
    per_dest = local_experts * capacity
    table = route_table(routes, experts_all, capacity)
    slot_tokens, slot_cot, slot_gates = dispatch(table, tokens, cotangent, gates)
    slot_tokens = slot_tokens.reshape(n_expert, per_dest, width)
    slot_cot = slot_cot.reshape(n_expert, per_dest, width)
    slot_gates = slot_gates.reshape(n_expert, per_dest)
    recv_tokens, recv_cot, recv_gates = (
        lax.all_to_all(slot_tokens, "expert", split_axis=0, concat_axis=0, tiled=True),
        lax.all_to_all(slot_cot, "expert", split_axis=0, concat_axis=0, tiled=True),
        lax.all_to_all(slot_gates, "expert", split_axis=0, concat_axis=0, tiled=True),
    )
    recv_tokens, recv_cot, recv_gates = (
        lax.all_gather(recv_tokens, "dp", axis=0, tiled=True),
        lax.all_gather(recv_cot, "dp", axis=0, tiled=True),
        lax.all_gather(recv_gates, "dp", axis=0, tiled=True),
    )
    rows = n_groups * n_expert
    token_part, gate_part, grad_gate, grad_up, grad_down = expert_work(
        recv_tokens.reshape(rows, local_experts, capacity, width),
        recv_cot.reshape(rows, local_experts, capacity, width),
        recv_gates.reshape(rows, local_experts, capacity),
        w_gate,
        w_up,
        w_down,
    )
    token_part = token_part.reshape(n_groups, n_expert * per_dest, width)
    gate_part = gate_part.reshape(n_groups, n_expert * per_dest)
    token_part, gate_part = (
        lax.psum_scatter(token_part, "dp", scatter_dimension=0, tiled=False),
        lax.psum_scatter(gate_part, "dp", scatter_dimension=0, tiled=False),
    )
    token_part = token_part.reshape(n_expert, per_dest, width)
    gate_part = gate_part.reshape(n_expert, per_dest)
    back_tokens, back_gates = (
        lax.all_to_all(token_part, "expert", split_axis=0, concat_axis=0, tiled=True),
        lax.all_to_all(gate_part, "expert", split_axis=0, concat_axis=0, tiled=True),
    )
    back_tokens = back_tokens.reshape(slots, width)
    back_gates = back_gates.reshape(slots)
    spread = table.reshape(tok_count, TOPK, slots).sum(axis=1)
    token_sum = jnp.einsum("ts,sd->td", spread, back_tokens, precision=lax.Precision.HIGHEST)
    gate_sum = jnp.einsum("ps,s->p", table, back_gates, precision=lax.Precision.HIGHEST)
    token_grads = token_sum.astype(jnp.bfloat16)
    gate_grads = gate_sum.reshape(tok_count, TOPK)
    return (token_grads, gate_grads, grad_gate, grad_up, grad_down)


def solution(mesh):
    return jax.shard_map(
        local,
        mesh=mesh,
        in_specs=(
            P(("dp", "expert"), None),
            P(("dp", "expert"), None),
            P(("dp", "expert"), None),
            P(("dp", "expert"), None),
            P("expert", None, "dp"),
            P("expert", None, "dp"),
            P("expert", "dp", None),
        ),
        out_specs=(
            P(("dp", "expert"), None),
            P(("dp", "expert"), None),
            P("expert", None, "dp"),
            P("expert", None, "dp"),
            P("expert", "dp", None),
        ),
        check_vma=False,
    )
```

```python
from functools import partial

import jax
import jax.numpy as jnp
from jax import lax
from jax.sharding import PartitionSpec as P

TOPK = 8


def route_table(routes, experts_all, capacity):
    pairs = routes.reshape(-1)
    onehot = (pairs[:, None] == jnp.arange(experts_all, dtype=jnp.int32)[None, :]).astype(jnp.int32)
    before = jnp.cumsum(onehot, axis=0) - onehot
    within = jnp.sum(before * onehot, axis=1)
    target = pairs * capacity + within
    slot_ids = jnp.arange(experts_all * capacity, dtype=jnp.int32)
    return (target[:, None] == slot_ids[None, :]).astype(jnp.float32)


def dispatch(table, tokens, cotangent, gates):
    count = tokens.shape[0]
    slots = table.shape[1]
    spread = table.reshape(count, TOPK, slots).sum(axis=1).astype(jnp.bfloat16)
    both = jnp.concatenate([tokens, cotangent], axis=1)
    slot_rows = jnp.einsum(
        "ts,td->sd", spread, both, preferred_element_type=jnp.float32
    ).astype(jnp.bfloat16)
    flat_gates = gates.reshape(-1).astype(jnp.float32)
    slot_gates = jnp.einsum("ps,p->s", table, flat_gates, precision=lax.Precision.HIGHEST).astype(
        jnp.bfloat16
    )
    pad = jnp.zeros((slots, 127), jnp.bfloat16)
    return jnp.concatenate([slot_rows, slot_gates[:, None], pad], axis=1)


def expert_one(rows_in, cot_in, row_gate, w_gate, w_up, w_down):
    gate_pre = jnp.dot(rows_in, w_gate, preferred_element_type=jnp.float32)
    upper_pre = jnp.dot(rows_in, w_up, preferred_element_type=jnp.float32)
    gate_sig = jax.nn.sigmoid(gate_pre)
    active = (gate_pre * gate_sig * upper_pre).astype(jnp.bfloat16)
    output = jnp.dot(active, w_down, preferred_element_type=jnp.float32)
    cot_float = cot_in.astype(jnp.float32)
    gate_part = jnp.sum(output * cot_float, axis=-1)
    scaled = (row_gate.astype(jnp.float32)[:, None] * cot_float).astype(jnp.bfloat16)
    grad_active = lax.dot_general(
        scaled, w_down, (((1,), (1,)), ((), ())), preferred_element_type=jnp.float32
    )
    grad_upper = (grad_active * gate_pre * gate_sig).astype(jnp.bfloat16)
    grad_gpre = (grad_active * upper_pre * gate_sig * (1.0 + gate_pre * (1.0 - gate_sig))).astype(
        jnp.bfloat16
    )
    token_part = lax.dot_general(
        grad_gpre, w_gate, (((1,), (1,)), ((), ())), preferred_element_type=jnp.float32
    )
    token_part = token_part + lax.dot_general(
        grad_upper, w_up, (((1,), (1,)), ((), ())), preferred_element_type=jnp.float32
    )
    grad_g = lax.dot_general(
        rows_in, grad_gpre, (((0,), (0,)), ((), ())), preferred_element_type=jnp.float32
    ).astype(jnp.bfloat16)
    grad_u = lax.dot_general(
        rows_in, grad_upper, (((0,), (0,)), ((), ())), preferred_element_type=jnp.float32
    ).astype(jnp.bfloat16)
    grad_d = lax.dot_general(
        active, scaled, (((0,), (0,)), ((), ())), preferred_element_type=jnp.float32
    ).astype(jnp.bfloat16)
    return (token_part, gate_part, grad_g, grad_u, grad_d)


def local(tokens, routes, gates, cotangent, w_gate, w_up, w_down):
    n_expert = lax.axis_size("expert")
    n_groups = lax.axis_size("dp")
    local_experts = w_gate.shape[0]
    experts_all = local_experts * n_expert
    tok_count = tokens.shape[0]
    width = tokens.shape[1]
    capacity = 16 * tok_count // experts_all
    slots = experts_all * capacity
    per_dest = local_experts * capacity
    table = route_table(routes, experts_all, capacity)
    send = dispatch(table, tokens, cotangent, gates)
    send = send.reshape(n_expert, per_dest, send.shape[-1])
    recv = lax.all_to_all(send, "expert", split_axis=0, concat_axis=0, tiled=True)
    recv = lax.all_gather(recv, "dp", axis=0, tiled=True)
    rows = n_groups * n_expert
    parts, gparts, grads_g, grads_u, grads_d = [], [], [], [], []
    for j in range(local_experts):
        block = recv[:, j * capacity:(j + 1) * capacity, :].reshape(rows * capacity, -1)
        token_part, gate_part, grad_g, grad_u, grad_d = expert_one(
            block[:, :width],
            block[:, width:2 * width],
            block[:, 2 * width],
            w_gate[j],
            w_up[j],
            w_down[j],
        )
        token_part = token_part.reshape(n_groups, n_expert * capacity, width)
        part = lax.psum_scatter(token_part, "dp", scatter_dimension=0, tiled=False)
        parts.append(part.reshape(n_expert, capacity, width))
        gparts.append(gate_part.reshape(n_groups, n_expert, capacity))
        grads_g.append(grad_g)
        grads_u.append(grad_u)
        grads_d.append(grad_d)
    token_part = jnp.stack(parts, axis=1).reshape(n_expert, local_experts, capacity, width)
    gate_part = jnp.stack(gparts, axis=2).reshape(n_groups, n_expert * per_dest)
    gate_part = lax.psum_scatter(gate_part, "dp", scatter_dimension=0, tiled=False)
    gate_part = gate_part.reshape(n_expert, per_dest)
    back_tokens, back_gates = (
        lax.all_to_all(token_part, "expert", split_axis=0, concat_axis=0, tiled=True),
        lax.all_to_all(gate_part, "expert", split_axis=0, concat_axis=0, tiled=True),
    )
    back_tokens = back_tokens.reshape(slots, width)
    back_gates = back_gates.reshape(slots)
    spread = table.reshape(tok_count, TOPK, slots).sum(axis=1)
    token_sum = jnp.einsum("ts,sd->td", spread, back_tokens, precision=lax.Precision.HIGHEST)
    gate_sum = jnp.einsum("ps,s->p", table, back_gates, precision=lax.Precision.HIGHEST)
    token_grads = token_sum.astype(jnp.bfloat16)
    gate_grads = gate_sum.reshape(tok_count, TOPK)
    grad_gate = jnp.stack(grads_g, axis=0)
    grad_up = jnp.stack(grads_u, axis=0)
    grad_down = jnp.stack(grads_d, axis=0)
    return (token_grads, gate_grads, grad_gate, grad_up, grad_down)


def solution(mesh):
    return jax.shard_map(
        local,
        mesh=mesh,
        in_specs=(
            P(("dp", "expert"), None),
            P(("dp", "expert"), None),
            P(("dp", "expert"), None),
            P(("dp", "expert"), None),
            P("expert", None, "dp"),
            P("expert", None, "dp"),
            P("expert", "dp", None),
        ),
        out_specs=(
            P(("dp", "expert"), None),
            P(("dp", "expert"), None),
            P("expert", None, "dp"),
            P("expert", None, "dp"),
            P("expert", "dp", None),
        ),
        check_vma=False,
    )
```

```python
from functools import partial

import jax
import jax.numpy as jnp
from jax import lax
from jax.sharding import PartitionSpec as P

TOPK = 8


def route_table(routes, experts_all, capacity):
    pairs = routes.reshape(-1)
    onehot = (pairs[:, None] == jnp.arange(experts_all, dtype=jnp.int32)[None, :]).astype(jnp.int32)
    before = jnp.cumsum(onehot, axis=0) - onehot
    within = jnp.sum(before * onehot, axis=1)
    target = pairs * capacity + within
    slot_ids = jnp.arange(experts_all * capacity, dtype=jnp.int32)
    return (target[:, None] == slot_ids[None, :]).astype(jnp.float32)


def dispatch(table, tokens, cotangent, gates):
    count = tokens.shape[0]
    slots = table.shape[1]
    spread = table.reshape(count, TOPK, slots).sum(axis=1).astype(jnp.bfloat16)
    both = jnp.concatenate([tokens, cotangent], axis=1)
    slot_rows = jnp.einsum(
        "ts,td->sd", spread, both, preferred_element_type=jnp.float32
    ).astype(jnp.bfloat16)
    flat_gates = gates.reshape(-1).astype(jnp.float32)
    slot_gates = jnp.einsum("ps,p->s", table, flat_gates, precision=lax.Precision.HIGHEST).astype(
        jnp.bfloat16
    )
    pad = jnp.zeros((slots, 127), jnp.bfloat16)
    return jnp.concatenate([slot_rows, slot_gates[:, None], pad], axis=1)


def expert_work(recv, w_gate, w_up, w_down, width, capacity):
    rows = recv.shape[0]
    local_experts = w_gate.shape[0]
    blocks = recv.reshape(rows, local_experts, capacity, recv.shape[-1])
    slot_tokens = blocks[..., :width]
    slot_cot = blocks[..., width:2 * width]
    slot_gates = blocks[..., 2 * width]
    gate_pre = jnp.einsum("rjcd,jdh->rjch", slot_tokens, w_gate, preferred_element_type=jnp.float32)
    upper_pre = jnp.einsum("rjcd,jdh->rjch", slot_tokens, w_up, preferred_element_type=jnp.float32)
    gate_sig = jax.nn.sigmoid(gate_pre)
    active = (gate_pre * gate_sig * upper_pre).astype(jnp.bfloat16)
    output = jnp.einsum("rjch,jhd->rjcd", active, w_down, preferred_element_type=jnp.float32)
    cot_float = slot_cot.astype(jnp.float32)
    gate_part = jnp.sum(output * cot_float, axis=-1)
    scaled = (slot_gates.astype(jnp.float32)[..., None] * cot_float).astype(jnp.bfloat16)
    grad_active = jnp.einsum("rjcd,jhd->rjch", scaled, w_down, preferred_element_type=jnp.float32)
    grad_upper = (grad_active * gate_pre * gate_sig).astype(jnp.bfloat16)
    grad_gpre = (grad_active * upper_pre * gate_sig * (1.0 + gate_pre * (1.0 - gate_sig))).astype(
        jnp.bfloat16
    )
    grad_g = jnp.einsum(
        "rjcd,rjch->jdh", slot_tokens, grad_gpre, preferred_element_type=jnp.float32
    ).astype(jnp.bfloat16)
    grad_u = jnp.einsum(
        "rjcd,rjch->jdh", slot_tokens, grad_upper, preferred_element_type=jnp.float32
    ).astype(jnp.bfloat16)
    grad_d = jnp.einsum(
        "rjch,rjcd->jhd", active, scaled, preferred_element_type=jnp.float32
    ).astype(jnp.bfloat16)
    parts = []
    for j in range(local_experts):
        gpre_j = grad_gpre[:, j].reshape(rows * capacity, -1)
        upper_j = grad_upper[:, j].reshape(rows * capacity, -1)
        token_part = lax.dot_general(
            gpre_j, w_gate[j], (((1,), (1,)), ((), ())), preferred_element_type=jnp.float32
        )
        token_part = token_part + lax.dot_general(
            upper_j, w_up[j], (((1,), (1,)), ((), ())), preferred_element_type=jnp.float32
        )
        gate_col = gate_part[:, j].reshape(rows * capacity, 1)
        pad = jnp.zeros((rows * capacity, 127), jnp.float32)
        parts.append(jnp.concatenate([token_part, gate_col, pad], axis=1))
    return (parts, grad_g, grad_u, grad_d)


def local(tokens, routes, gates, cotangent, w_gate, w_up, w_down):
    n_expert = lax.axis_size("expert")
    n_groups = lax.axis_size("dp")
    local_experts = w_gate.shape[0]
    experts_all = local_experts * n_expert
    tok_count = tokens.shape[0]
    width = tokens.shape[1]
    capacity = 16 * tok_count // experts_all
    slots = experts_all * capacity
    per_dest = local_experts * capacity
    table = route_table(routes, experts_all, capacity)
    send = dispatch(table, tokens, cotangent, gates)
    send = send.reshape(n_expert, per_dest, send.shape[-1])
    recv = lax.all_to_all(send, "expert", split_axis=0, concat_axis=0, tiled=True)
    recv = lax.all_gather(recv, "dp", axis=0, tiled=True)
    parts, grad_gate, grad_up, grad_down = expert_work(recv, w_gate, w_up, w_down, width, capacity)
    wide = parts[0].shape[-1]
    summed = []
    for part in parts:
        part = part.reshape(n_groups, n_expert * capacity, wide)
        part = lax.psum_scatter(part, "dp", scatter_dimension=0, tiled=False)
        summed.append(part.reshape(n_expert, capacity, wide))
    back = jnp.stack(summed, axis=1)
    back = lax.all_to_all(back, "expert", split_axis=0, concat_axis=0, tiled=True)
    back = back.reshape(slots, wide)
    back_tokens = back[:, :width]
    back_gates = back[:, width]
    spread = table.reshape(tok_count, TOPK, slots).sum(axis=1)
    token_sum = jnp.einsum("ts,sd->td", spread, back_tokens, precision=lax.Precision.HIGHEST)
    gate_sum = jnp.einsum("ps,s->p", table, back_gates, precision=lax.Precision.HIGHEST)
    token_grads = token_sum.astype(jnp.bfloat16)
    gate_grads = gate_sum.reshape(tok_count, TOPK)
    return (token_grads, gate_grads, grad_gate, grad_up, grad_down)


def solution(mesh):
    return jax.shard_map(
        local,
        mesh=mesh,
        in_specs=(
            P(("dp", "expert"), None),
            P(("dp", "expert"), None),
            P(("dp", "expert"), None),
            P(("dp", "expert"), None),
            P("expert", None, "dp"),
            P("expert", None, "dp"),
            P("expert", "dp", None),
        ),
        out_specs=(
            P(("dp", "expert"), None),
            P(("dp", "expert"), None),
            P("expert", None, "dp"),
            P("expert", None, "dp"),
            P("expert", "dp", None),
        ),
        check_vma=False,
    )
```

```python
from functools import partial

import jax
import jax.numpy as jnp
from jax import lax
from jax.sharding import PartitionSpec as P

TOPK = 8


def route_table(routes, experts_all, capacity):
    pairs = routes.reshape(-1)
    onehot = (pairs[:, None] == jnp.arange(experts_all, dtype=jnp.int32)[None, :]).astype(jnp.int32)
    before = jnp.cumsum(onehot, axis=0) - onehot
    within = jnp.sum(before * onehot, axis=1)
    target = pairs * capacity + within
    slot_ids = jnp.arange(experts_all * capacity, dtype=jnp.int32)
    return (target[:, None] == slot_ids[None, :]).astype(jnp.float32)


def dispatch(table, tokens, cotangent, gates):
    count = tokens.shape[0]
    slots = table.shape[1]
    spread = table.reshape(count, TOPK, slots).sum(axis=1).astype(jnp.bfloat16)
    both = jnp.concatenate([tokens, cotangent], axis=1)
    slot_rows = jnp.einsum(
        "ts,td->sd", spread, both, preferred_element_type=jnp.float32
    ).astype(jnp.bfloat16)
    flat_gates = gates.reshape(-1).astype(jnp.float32)
    slot_gates = jnp.einsum("ps,p->s", table, flat_gates, precision=lax.Precision.HIGHEST).astype(
        jnp.bfloat16
    )
    pad = jnp.zeros((slots, 127), jnp.bfloat16)
    return jnp.concatenate([slot_rows, slot_gates[:, None], pad], axis=1)


def expert_one(rows_in, cot_in, row_gate, w_gate, w_up, w_down):
    gate_pre = jnp.dot(rows_in, w_gate, preferred_element_type=jnp.float32)
    upper_pre = jnp.dot(rows_in, w_up, preferred_element_type=jnp.float32)
    gate_sig = jax.nn.sigmoid(gate_pre)
    active = (gate_pre * gate_sig * upper_pre).astype(jnp.bfloat16)
    output = jnp.dot(active, w_down, preferred_element_type=jnp.float32)
    cot_float = cot_in.astype(jnp.float32)
    gate_part = jnp.sum(output * cot_float, axis=-1)
    scaled = (row_gate.astype(jnp.float32)[:, None] * cot_float).astype(jnp.bfloat16)
    grad_active = lax.dot_general(
        scaled, w_down, (((1,), (1,)), ((), ())), preferred_element_type=jnp.float32
    )
    grad_upper = (grad_active * gate_pre * gate_sig).astype(jnp.bfloat16)
    grad_gpre = (grad_active * upper_pre * gate_sig * (1.0 + gate_pre * (1.0 - gate_sig))).astype(
        jnp.bfloat16
    )
    token_part = lax.dot_general(
        grad_gpre, w_gate, (((1,), (1,)), ((), ())), preferred_element_type=jnp.float32
    )
    token_part = token_part + lax.dot_general(
        grad_upper, w_up, (((1,), (1,)), ((), ())), preferred_element_type=jnp.float32
    )
    grad_g = lax.dot_general(
        rows_in, grad_gpre, (((0,), (0,)), ((), ())), preferred_element_type=jnp.float32
    ).astype(jnp.bfloat16)
    grad_u = lax.dot_general(
        rows_in, grad_upper, (((0,), (0,)), ((), ())), preferred_element_type=jnp.float32
    ).astype(jnp.bfloat16)
    grad_d = lax.dot_general(
        active, scaled, (((0,), (0,)), ((), ())), preferred_element_type=jnp.float32
    ).astype(jnp.bfloat16)
    return (token_part, gate_part, grad_g, grad_u, grad_d)


def local(tokens, routes, gates, cotangent, w_gate, w_up, w_down):
    n_expert = lax.axis_size("expert")
    n_groups = lax.axis_size("dp")
    local_experts = w_gate.shape[0]
    experts_all = local_experts * n_expert
    tok_count = tokens.shape[0]
    width = tokens.shape[1]
    capacity = 16 * tok_count // experts_all
    slots = experts_all * capacity
    table = route_table(routes, experts_all, capacity)
    send = dispatch(table, tokens, cotangent, gates)
    send = send.reshape(n_expert, local_experts, capacity, send.shape[-1])
    rows = n_groups * n_expert
    summed, grads_g, grads_u, grads_d = [], [], [], []
    for j in range(local_experts):
        piece = send[:, j].reshape(n_expert * capacity, send.shape[-1])
        recv = lax.all_to_all(piece, "expert", split_axis=0, concat_axis=0, tiled=True)
        block = lax.all_gather(recv, "dp", axis=0, tiled=True)
        token_part, gate_part, grad_g, grad_u, grad_d = expert_one(
            block[:, :width],
            block[:, width:2 * width],
            block[:, 2 * width],
            w_gate[j],
            w_up[j],
            w_down[j],
        )
        pad = jnp.zeros((rows * capacity, 127), jnp.float32)
        part = jnp.concatenate([token_part, gate_part[:, None], pad], axis=1)
        wide = part.shape[-1]
        part = part.reshape(n_groups, n_expert * capacity, wide)
        part = lax.psum_scatter(part, "dp", scatter_dimension=0, tiled=False)
        summed.append(part.reshape(n_expert, capacity, wide))
        grads_g.append(grad_g)
        grads_u.append(grad_u)
        grads_d.append(grad_d)
    back = jnp.stack(summed, axis=1)
    back = lax.all_to_all(back, "expert", split_axis=0, concat_axis=0, tiled=True)
    back = back.reshape(slots, back.shape[-1])
    back_tokens = back[:, :width]
    back_gates = back[:, width]
    spread = table.reshape(tok_count, TOPK, slots).sum(axis=1)
    token_sum = jnp.einsum("ts,sd->td", spread, back_tokens, precision=lax.Precision.HIGHEST)
    gate_sum = jnp.einsum("ps,s->p", table, back_gates, precision=lax.Precision.HIGHEST)
    token_grads = token_sum.astype(jnp.bfloat16)
    gate_grads = gate_sum.reshape(tok_count, TOPK)
    grad_gate = jnp.stack(grads_g, axis=0)
    grad_up = jnp.stack(grads_u, axis=0)
    grad_down = jnp.stack(grads_d, axis=0)
    return (token_grads, gate_grads, grad_gate, grad_up, grad_down)


def solution(mesh):
    return jax.shard_map(
        local,
        mesh=mesh,
        in_specs=(
            P(("dp", "expert"), None),
            P(("dp", "expert"), None),
            P(("dp", "expert"), None),
            P(("dp", "expert"), None),
            P("expert", None, "dp"),
            P("expert", None, "dp"),
            P("expert", "dp", None),
        ),
        out_specs=(
            P(("dp", "expert"), None),
            P(("dp", "expert"), None),
            P("expert", None, "dp"),
            P("expert", None, "dp"),
            P("expert", "dp", None),
        ),
        check_vma=False,
    )
```

```python
from functools import partial

import jax
import jax.numpy as jnp
from jax import lax
from jax.sharding import PartitionSpec as P

TOPK = 8


def route_table(routes, experts_all, capacity):
    pairs = routes.reshape(-1)
    onehot = (pairs[:, None] == jnp.arange(experts_all, dtype=jnp.int32)[None, :]).astype(jnp.int32)
    before = jnp.cumsum(onehot, axis=0) - onehot
    within = jnp.sum(before * onehot, axis=1)
    target = pairs * capacity + within
    slot_ids = jnp.arange(experts_all * capacity, dtype=jnp.int32)
    return (target[:, None] == slot_ids[None, :]).astype(jnp.float32)


def dispatch(table, tokens, cotangent, gates):
    count = tokens.shape[0]
    slots = table.shape[1]
    spread = table.reshape(count, TOPK, slots).sum(axis=1).astype(jnp.bfloat16)
    both = jnp.concatenate([tokens, cotangent], axis=1)
    slot_rows = jnp.einsum(
        "ts,td->sd", spread, both, preferred_element_type=jnp.float32
    ).astype(jnp.bfloat16)
    flat_gates = gates.reshape(-1).astype(jnp.float32)
    slot_gates = jnp.einsum("ps,p->s", table, flat_gates, precision=lax.Precision.HIGHEST).astype(
        jnp.bfloat16
    )
    pad = jnp.zeros((slots, 127), jnp.bfloat16)
    return jnp.concatenate([slot_rows, slot_gates[:, None], pad], axis=1)


def expert_one(rows_in, cot_in, row_gate, w_gate, w_up, w_down):
    gate_pre = jnp.dot(rows_in, w_gate, preferred_element_type=jnp.float32)
    upper_pre = jnp.dot(rows_in, w_up, preferred_element_type=jnp.float32)
    gate_sig = jax.nn.sigmoid(gate_pre)
    active = (gate_pre * gate_sig * upper_pre).astype(jnp.bfloat16)
    output = jnp.dot(active, w_down, preferred_element_type=jnp.float32)
    cot_float = cot_in.astype(jnp.float32)
    gate_part = jnp.sum(output * cot_float, axis=-1)
    scaled = (row_gate.astype(jnp.float32)[:, None] * cot_float).astype(jnp.bfloat16)
    grad_active = lax.dot_general(
        scaled, w_down, (((1,), (1,)), ((), ())), preferred_element_type=jnp.float32
    )
    grad_upper = (grad_active * gate_pre * gate_sig).astype(jnp.bfloat16)
    grad_gpre = (grad_active * upper_pre * gate_sig * (1.0 + gate_pre * (1.0 - gate_sig))).astype(
        jnp.bfloat16
    )
    token_part = lax.dot_general(
        grad_gpre, w_gate, (((1,), (1,)), ((), ())), preferred_element_type=jnp.float32
    )
    token_part = token_part + lax.dot_general(
        grad_upper, w_up, (((1,), (1,)), ((), ())), preferred_element_type=jnp.float32
    )
    grad_g = lax.dot_general(
        rows_in, grad_gpre, (((0,), (0,)), ((), ())), preferred_element_type=jnp.float32
    ).astype(jnp.bfloat16)
    grad_u = lax.dot_general(
        rows_in, grad_upper, (((0,), (0,)), ((), ())), preferred_element_type=jnp.float32
    ).astype(jnp.bfloat16)
    grad_d = lax.dot_general(
        active, scaled, (((0,), (0,)), ((), ())), preferred_element_type=jnp.float32
    ).astype(jnp.bfloat16)
    return (token_part, gate_part, grad_g, grad_u, grad_d)


def local(tokens, routes, gates, cotangent, w_gate, w_up, w_down):
    n_expert = lax.axis_size("expert")
    n_groups = lax.axis_size("dp")
    local_experts = w_gate.shape[0]
    experts_all = local_experts * n_expert
    tok_count = tokens.shape[0]
    width = tokens.shape[1]
    capacity = 16 * tok_count // experts_all
    slots = experts_all * capacity
    table = route_table(routes, experts_all, capacity)
    send = dispatch(table, tokens, cotangent, gates)
    send = send.reshape(n_expert, local_experts, capacity, send.shape[-1])
    rows = n_groups * n_expert
    summed, grads_g, grads_u, grads_d = [], [], [], []
    for j in range(local_experts):
        piece = send[:, j].reshape(n_expert * capacity, send.shape[-1])
        recv = lax.all_to_all(piece, "expert", split_axis=0, concat_axis=0, tiled=True)
        block = lax.all_gather(recv, "dp", axis=0, tiled=True)
        token_part, gate_part, grad_g, grad_u, grad_d = expert_one(
            block[:, :width],
            block[:, width:2 * width],
            block[:, 2 * width],
            w_gate[j],
            w_up[j],
            w_down[j],
        )
        pad = jnp.zeros((rows * capacity, 127), jnp.float32)
        part = jnp.concatenate([token_part, gate_part[:, None], pad], axis=1)
        wide = part.shape[-1]
        part = part.reshape(n_groups, n_expert * capacity, wide)
        part = lax.psum_scatter(part.astype(jnp.bfloat16), "dp", scatter_dimension=0, tiled=False)
        summed.append(part.astype(jnp.float32).reshape(n_expert, capacity, wide))
        grads_g.append(grad_g)
        grads_u.append(grad_u)
        grads_d.append(grad_d)
    back = jnp.stack(summed, axis=1)
    back = lax.all_to_all(back, "expert", split_axis=0, concat_axis=0, tiled=True)
    back = back.reshape(slots, back.shape[-1])
    back_tokens = back[:, :width]
    back_gates = back[:, width]
    spread = table.reshape(tok_count, TOPK, slots).sum(axis=1)
    token_sum = jnp.einsum("ts,sd->td", spread, back_tokens, precision=lax.Precision.HIGHEST)
    gate_sum = jnp.einsum("ps,s->p", table, back_gates, precision=lax.Precision.HIGHEST)
    token_grads = token_sum.astype(jnp.bfloat16)
    gate_grads = gate_sum.reshape(tok_count, TOPK)
    grad_gate = jnp.stack(grads_g, axis=0)
    grad_up = jnp.stack(grads_u, axis=0)
    grad_down = jnp.stack(grads_d, axis=0)
    return (token_grads, gate_grads, grad_gate, grad_up, grad_down)


def solution(mesh):
    return jax.shard_map(
        local,
        mesh=mesh,
        in_specs=(
            P(("dp", "expert"), None),
            P(("dp", "expert"), None),
            P(("dp", "expert"), None),
            P(("dp", "expert"), None),
            P("expert", None, "dp"),
            P("expert", None, "dp"),
            P("expert", "dp", None),
        ),
        out_specs=(
            P(("dp", "expert"), None),
            P(("dp", "expert"), None),
            P("expert", None, "dp"),
            P("expert", None, "dp"),
            P("expert", "dp", None),
        ),
        check_vma=False,
    )
```

```python
from functools import partial

import jax
import jax.numpy as jnp
from jax import lax
from jax.sharding import PartitionSpec as P

TOPK = 8


def route_table(routes, experts_all, capacity):
    pairs = routes.reshape(-1)
    onehot = (pairs[:, None] == jnp.arange(experts_all, dtype=jnp.int32)[None, :]).astype(jnp.int32)
    before = jnp.cumsum(onehot, axis=0) - onehot
    within = jnp.sum(before * onehot, axis=1)
    target = pairs * capacity + within
    slot_ids = jnp.arange(experts_all * capacity, dtype=jnp.int32)
    return (target[:, None] == slot_ids[None, :]).astype(jnp.float32)


def dispatch(table, tokens, cotangent, gates):
    count = tokens.shape[0]
    slots = table.shape[1]
    spread = table.reshape(count, TOPK, slots).sum(axis=1).astype(jnp.bfloat16)
    both = jnp.concatenate([tokens, cotangent], axis=1)
    slot_rows = jnp.einsum(
        "ts,td->sd", spread, both, preferred_element_type=jnp.float32
    ).astype(jnp.bfloat16)
    flat_gates = gates.reshape(-1).astype(jnp.float32)
    slot_gates = jnp.einsum("ps,p->s", table, flat_gates, precision=lax.Precision.HIGHEST).astype(
        jnp.bfloat16
    )
    pad = jnp.zeros((slots, 127), jnp.bfloat16)
    return jnp.concatenate([slot_rows, slot_gates[:, None], pad], axis=1)


def expert_one(rows_in, cot_in, row_gate, w_gate, w_up, w_down):
    gate_pre = jnp.dot(rows_in, w_gate, preferred_element_type=jnp.float32)
    upper_pre = jnp.dot(rows_in, w_up, preferred_element_type=jnp.float32)
    gate_sig = jax.nn.sigmoid(gate_pre)
    active = (gate_pre * gate_sig * upper_pre).astype(jnp.bfloat16)
    output = jnp.dot(active, w_down, preferred_element_type=jnp.float32)
    cot_float = cot_in.astype(jnp.float32)
    gate_part = jnp.sum(output * cot_float, axis=-1)
    scaled = (row_gate.astype(jnp.float32)[:, None] * cot_float).astype(jnp.bfloat16)
    grad_active = lax.dot_general(
        scaled, w_down, (((1,), (1,)), ((), ())), preferred_element_type=jnp.float32
    )
    grad_upper = (grad_active * gate_pre * gate_sig).astype(jnp.bfloat16)
    grad_gpre = (grad_active * upper_pre * gate_sig * (1.0 + gate_pre * (1.0 - gate_sig))).astype(
        jnp.bfloat16
    )
    token_part = lax.dot_general(
        grad_gpre, w_gate, (((1,), (1,)), ((), ())), preferred_element_type=jnp.float32
    )
    token_part = token_part + lax.dot_general(
        grad_upper, w_up, (((1,), (1,)), ((), ())), preferred_element_type=jnp.float32
    )
    grad_g = lax.dot_general(
        rows_in, grad_gpre, (((0,), (0,)), ((), ())), preferred_element_type=jnp.float32
    ).astype(jnp.bfloat16)
    grad_u = lax.dot_general(
        rows_in, grad_upper, (((0,), (0,)), ((), ())), preferred_element_type=jnp.float32
    ).astype(jnp.bfloat16)
    grad_d = lax.dot_general(
        active, scaled, (((0,), (0,)), ((), ())), preferred_element_type=jnp.float32
    ).astype(jnp.bfloat16)
    return (token_part, gate_part, grad_g, grad_u, grad_d)


def local(tokens, routes, gates, cotangent, w_gate, w_up, w_down):
    n_expert = lax.axis_size("expert")
    n_groups = lax.axis_size("dp")
    local_experts = w_gate.shape[0]
    experts_all = local_experts * n_expert
    tok_count = tokens.shape[0]
    width = tokens.shape[1]
    capacity = 16 * tok_count // experts_all
    slots = experts_all * capacity
    table = route_table(routes, experts_all, capacity)
    send = dispatch(table, tokens, cotangent, gates)
    send = send.reshape(n_expert, local_experts, capacity, send.shape[-1])
    rows = n_groups * n_expert
    summed, grads_g, grads_u, grads_d = [], [], [], []
    for j in range(local_experts):
        piece = send[:, j].reshape(n_expert * capacity, send.shape[-1])
        recv = lax.all_to_all(piece, "expert", split_axis=0, concat_axis=0, tiled=True)
        block = lax.all_gather(recv, "dp", axis=0, tiled=True)
        token_part, gate_part, grad_g, grad_u, grad_d = expert_one(
            block[:, :width],
            block[:, width:2 * width],
            block[:, 2 * width],
            w_gate[j],
            w_up[j],
            w_down[j],
        )
        pad = jnp.zeros((rows * capacity, 127), jnp.float32)
        part = jnp.concatenate([token_part, gate_part[:, None], pad], axis=1)
        wide = part.shape[-1]
        part = part.reshape(n_groups, n_expert * capacity, wide)
        part = lax.psum_scatter(part, "dp", scatter_dimension=0, tiled=False)
        part = part.reshape(n_expert, capacity, wide)
        summed.append(lax.all_to_all(part, "expert", split_axis=0, concat_axis=0, tiled=True))
        grads_g.append(grad_g)
        grads_u.append(grad_u)
        grads_d.append(grad_d)
    back = jnp.stack(summed, axis=1)
    back = back.reshape(slots, back.shape[-1])
    back_tokens = back[:, :width]
    back_gates = back[:, width]
    spread = table.reshape(tok_count, TOPK, slots).sum(axis=1)
    token_sum = jnp.einsum("ts,sd->td", spread, back_tokens, precision=lax.Precision.HIGHEST)
    gate_sum = jnp.einsum("ps,s->p", table, back_gates, precision=lax.Precision.HIGHEST)
    token_grads = token_sum.astype(jnp.bfloat16)
    gate_grads = gate_sum.reshape(tok_count, TOPK)
    grad_gate = jnp.stack(grads_g, axis=0)
    grad_up = jnp.stack(grads_u, axis=0)
    grad_down = jnp.stack(grads_d, axis=0)
    return (token_grads, gate_grads, grad_gate, grad_up, grad_down)


def solution(mesh):
    return jax.shard_map(
        local,
        mesh=mesh,
        in_specs=(
            P(("dp", "expert"), None),
            P(("dp", "expert"), None),
            P(("dp", "expert"), None),
            P(("dp", "expert"), None),
            P("expert", None, "dp"),
            P("expert", None, "dp"),
            P("expert", "dp", None),
        ),
        out_specs=(
            P(("dp", "expert"), None),
            P(("dp", "expert"), None),
            P("expert", None, "dp"),
            P("expert", None, "dp"),
            P("expert", "dp", None),
        ),
        check_vma=False,
    )
```
